1024 devices in a mesh: sub: 128 (over z, y), grp: 8 (over x, core).
Axes of the slice: x: 4, y: 8, z: 16, core: 2. Of those that a mesh axis runs over, the one named last changes fastest.
Arguments:
- rhs: float32 [262144, 512], P(('sub', 'grp')), may hold values from -120 to 120
- kappa: float32 [262144], P(('sub', 'grp')), may hold values from 0.5 to 5
- stiffness: float32 [512, 512], replicated, may hold values from -1 to 3
- local_inverse: float32 [512, 512], replicated, may hold values from -1 to 2
- modes: float32 [8, 512], replicated, may hold values from -0.25 to 0.25
- coarse_weight: float32 [8, 262144], P(None, ('sub', 'grp')), may hold values from 0.5 to 1.5
- coarse_mask: int32 [8, 262144], P(None, ('sub', 'grp')), may hold values 0 or 1
- coarse_inverse: float32 [8192, 8192], P(('sub', 'grp')), may hold values from -1 to 1
- neighbours: int32 [4, 262144], P(None, ('sub', 'grp')), may hold values from -1 to 262143, as said below
Outputs:
- solution: float32 [262144, 512], P(('sub', 'grp'))
The draws below stay inside these ranges and needn't reach their ends.
Inputs may be any that keep to these rules, and one draw needn't show every extreme that they name: `neighbours`: entries are element numbers or -1. For element e of subdomain d (elements d * 256 to d * 256 + 255), rows 0 and 1 name two other elements of subdomain d, row 2 names an element of subdomain d - 8 or -1, row 3 an element of subdomain d + 8 or -1. Every relation is mutual: row 0 of a names b exactly where row 1 of b names a, and row 3 of a names b exactly where row 2 of b names a. Between subdomains d and d + 8 there are 1 to 64 linked pairs, exactly 64 for some d.
All inputs are finite; a program needn't handle non-finite values. No bound on the sum of `coarse_mask` on one device may be relied on, other than what follows from the above.
Results may differ from the reference program's by a relative error of at most 0.000093.
Values sent between devices are 32-bit elements; how exact they have to be, the bound alone decides.
No kernel may reach another device: no remote copies, remote signals or barrier semaphores. Data moves between devices by JAX's collectives and lax.ppermute only.
A program may use at most 32 MiB of HBM per device.

```python
import math
import jax
import jax.numpy as jnp
from jax import lax

NP = 512
FACE = 64
E_DEV = 256
BND = 64
CDEV = 8
GROUPS = 8
DOMAINS = 1024
NE = 262144
NC = 8192


def dominant_matrix(key, order, low, high, spread):
    k_diag, k_off = jax.random.split(key)
    diagonal = jnp.exp(jax.random.uniform(k_diag, (order,), jnp.float32, math.log(low), math.log(high)))
    off = jnp.clip(jax.random.normal(k_off, (order, order), jnp.float32), -4.0, 4.0)
    places = jnp.arange(order)
    on_diagonal = places[:, None] == places[None, :]
    return jnp.where(on_diagonal, diagonal[None, :], off * (spread / order ** 0.5))


def draw_stiffness(key, part):
    return dominant_matrix(jax.random.fold_in(key, 1), NP, 1.0, 3.0, 0.5)


def draw_local_inverse(key, part):
    return dominant_matrix(jax.random.fold_in(key, 2), NP, 0.4, 1.2, 0.3)


def draw_coarse_inverse(key, part):
    return dominant_matrix(jax.random.fold_in(key, 3), NC, 0.05, 0.5, 0.05)


def draw_rhs(key, part):
    k_val, k_row = jax.random.split(jax.random.fold_in(key, 4), 2)
    place = jnp.arange(NE, dtype=jnp.float32) / NE
    ramp = jnp.exp(math.log(3.0) * place)
    rows = jnp.exp(jax.random.uniform(k_row, (NE,), jnp.float32, 0.0, math.log(10.0)))
    values = jnp.clip(jax.random.normal(k_val, (NE, NP), jnp.float32), -4.0, 4.0)
    return values * (ramp * rows)[:, None]


def draw_neighbours(key, part):
    devices = NE // E_DEV
    links = devices - GROUPS
    k_cycle, k_count, k_top, k_low, k_high = jax.random.split(jax.random.fold_in(key, 5), 5)
    cycle = jax.vmap(lambda k: jax.random.permutation(k, E_DEV))(jax.random.split(k_cycle, devices)).astype(jnp.int32)
    where_in = jnp.argsort(cycle, axis=1)
    before = jnp.roll(cycle, 1, axis=1)
    after = jnp.roll(cycle, -1, axis=1)
    base = (jnp.arange(devices, dtype=jnp.int32) * E_DEV)[:, None]
    first = base + jnp.take_along_axis(before, where_in, 1)
    second = base + jnp.take_along_axis(after, where_in, 1)
    counts = jax.random.randint(k_count, (links,), 1, BND + 1)
    top = jax.random.randint(k_top, (), 0, links)
    counts = jnp.where(jnp.arange(links) == top, BND, counts)
    lower = jax.vmap(lambda k: jax.random.permutation(k, E_DEV))(jax.random.split(k_low, links)).astype(jnp.int32)
    upper = jax.vmap(lambda k: jax.random.permutation(k, E_DEV))(jax.random.split(k_high, links)).astype(jnp.int32)
    lower_rank = jnp.argsort(lower, axis=1)
    upper_rank = jnp.argsort(upper, axis=1)
    link_base = (jnp.arange(links, dtype=jnp.int32) * E_DEV)[:, None]
    partner_up = link_base + GROUPS * E_DEV + jnp.take_along_axis(upper, lower_rank, 1)
    up_side = jnp.where(lower_rank < counts[:, None], partner_up, -1)
    partner_down = link_base + jnp.take_along_axis(lower, upper_rank, 1)
    down_side = jnp.where(upper_rank < counts[:, None], partner_down, -1)
    empty = jnp.full((GROUPS, E_DEV), -1, jnp.int32)
    up_all = jnp.concatenate([up_side, empty], axis=0)
    down_all = jnp.concatenate([empty, down_side], axis=0)
    return jnp.stack([first, second, down_all, up_all]).reshape(4, NE).astype(jnp.int32)


def set_ends(result, key, low, top_value):
    spot = [jax.random.randint(jax.random.fold_in(key, axis), (), 0, length) for axis, length in enumerate(result.shape)]
    widest = result.shape.index(max(result.shape))
    next_to = spot[:widest] + [(spot[widest] + 1) % result.shape[widest]] + spot[widest + 1:]
    return result.at[tuple(spot)].set(low).at[tuple(next_to)].set(top_value)


def steps_of(rng, extent, shards, least, top_value):
    factor_of, own = 1.0, jax.random.fold_in(rng, 6)
    for dim, shards_of in shards:
        heights = jnp.exp(jax.random.uniform(jax.random.fold_in(own, dim), (shards_of,), jnp.float32, least / len(shards), top_value / len(shards)))
        factor_of = factor_of * jnp.repeat(heights, extent[dim] // shards_of).reshape([-1 if axis == dim else 1 for axis in range(len(extent))])
    return factor_of


def normal_values(key, shape, scale, reach, kind=jnp.bfloat16):
    drawn = jax.random.normal(key, shape, jnp.float32) * scale
    return jnp.minimum(jnp.maximum(drawn, -reach), reach).astype(kind)


def setup_inputs(seed: int = 0) -> dict:
    streams_of = jax.random.split(jax.random.key(seed), 10)
    rhs = draw_rhs(jax.random.fold_in(streams_of[9], 71), 0)
    kappa = jnp.clip(jnp.exp(math.log(5.0) - 2.3025851 * jax.random.uniform(streams_of[1], (NE,), jnp.float32) ** steps_of(streams_of[1], (NE,), ((0, 1024),), -0.2, 0.2)), 0.5, 5.0)
    stiffness = draw_stiffness(jax.random.fold_in(streams_of[9], 71), 0)
    local_inverse = draw_local_inverse(jax.random.fold_in(streams_of[9], 71), 0)
    modes = normal_values(streams_of[4], (CDEV, NP), NP ** -0.5, 0.25, jnp.float32)
    coarse_weight = jnp.clip(0.5 + 1.0 * jax.random.uniform(streams_of[5], (CDEV, NE), jnp.float32) ** steps_of(streams_of[5], (CDEV, NE), ((1, 1024),), -0.2, 0.2), 0.5, 1.5)
    coarse_mask = set_ends((jax.random.randint(streams_of[6], (CDEV, NE), 0, 2) < 1).astype(jnp.int32), jax.random.fold_in(streams_of[6], 1), 0, 1)
    coarse_inverse = draw_coarse_inverse(jax.random.fold_in(streams_of[9], 71), 0)
    neighbours = draw_neighbours(jax.random.fold_in(streams_of[9], 71), 0)
    return dict(rhs=rhs, kappa=kappa, stiffness=stiffness, local_inverse=local_inverse, modes=modes, coarse_weight=coarse_weight, coarse_mask=coarse_mask, coarse_inverse=coarse_inverse, neighbours=neighbours)


SIGMA = 1.0
HIGH = lax.Precision.HIGHEST

def operate(field, kappa, stiffness, neighbours):
    traces = jnp.concatenate([field[:, :FACE], field[:, NP - FACE:]], axis=1)
    valid = neighbours >= 0
    safe = jnp.where(valid, neighbours, 0).astype(jnp.int32)
    beside = jnp.zeros(traces.shape, jnp.float32)
    for slot in range(4):
        beside = beside + jnp.where(valid[slot][:, None], traces[safe[slot]], 0.0)
    degree = lax.optimization_barrier(jnp.sum(valid.astype(jnp.float32), axis=0))
    penalty = SIGMA * (degree[:, None] * traces - beside)
    middle = jnp.zeros((field.shape[0], NP - 2 * FACE), jnp.float32)
    lifted = jnp.concatenate([penalty[:, :FACE], middle, penalty[:, FACE:]], axis=1)
    return kappa[:, None] * jnp.dot(field, stiffness, precision=HIGH) + lifted

def precondition(residual, kappa, local_inverse, modes, weights, coarse_inverse):
    local_part = jnp.dot(residual, local_inverse, precision=HIGH) / kappa[:, None]
    projected = jnp.dot(modes, residual.T, precision=HIGH)
    restricted = lax.optimization_barrier(jnp.sum((weights * projected).reshape(CDEV, DOMAINS, E_DEV), axis=2)).T.reshape(NC)
    solved = jnp.dot(coarse_inverse, restricted, precision=HIGH)
    spread = jnp.repeat(solved.reshape(DOMAINS, CDEV).T, E_DEV, axis=1)
    coarse_part = jnp.dot((weights * spread).T, modes, precision=HIGH)
    return local_part + coarse_part

def reference(rhs, kappa, stiffness, local_inverse, modes, coarse_weight, coarse_mask, coarse_inverse, neighbours):
    weights = coarse_weight * coarse_mask.astype(jnp.float32)
    beta = jnp.sqrt(jnp.sum(rhs * rhs))
    first = rhs / beta
    z_one = precondition(first, kappa, local_inverse, modes, weights, coarse_inverse)
    w_one = operate(z_one, kappa, stiffness, neighbours)
    h11 = jnp.sum(w_one * first)
    s_one = jnp.sum(w_one * w_one)
    h21 = jnp.sqrt(s_one - h11 * h11)
    second = (w_one - h11 * first) / h21
    z_two = precondition(second, kappa, local_inverse, modes, weights, coarse_inverse)
    w_two = operate(z_two, kappa, stiffness, neighbours)
    h12 = jnp.sum(w_two * first)
    h22 = jnp.sum(w_two * second)
    s_two = jnp.sum(w_two * w_two)
    cross = h11 * h12 + h21 * h22
    det = s_one * s_two - cross * cross
    y_one = beta * (h11 * s_two - h12 * cross) / det
    y_two = beta * (h12 * s_one - h11 * cross) / det
    return y_one * z_one + y_two * z_two
```

```python
import functools

import jax
import jax.numpy as jnp
from jax import lax
from jax.experimental import pallas as pl
from jax.experimental.pallas import tpu as pltpu
from jax.sharding import PartitionSpec as P

FACE = 64
LANES = 128
KINDS = 8
SIGMA = 1.0
HIGH = lax.Precision.HIGHEST
F32 = jnp.float32
BF16 = jnp.bfloat16


def mm(a, b):
    return jnp.dot(a, b, precision=HIGH, preferred_element_type=F32)


def exact_left(small, value):
    high = value.astype(BF16)
    rest = value - high.astype(F32)
    middle = rest.astype(BF16)
    low = (rest - middle.astype(F32)).astype(BF16)
    width = value.shape[1]
    out = jnp.dot(
        small, jnp.concatenate([high, middle, low], axis=1), preferred_element_type=F32
    )
    return out[:, :width] + (out[:, width : 2 * width] + out[:, 2 * width :])


def total(values):
    return jnp.sum(jnp.sum(values, axis=0, keepdims=True), axis=1, keepdims=True)


def faces(field):
    return jnp.concatenate([field[:, :FACE], field[:, field.shape[1] - FACE :]], axis=1)


def slots(count, groups):
    odd = lax.rem(lax.axis_index("sub"), 2)
    place = lax.axis_index("grp") * KINDS
    return odd * (KINDS * groups) + place, (1 - odd) * (KINDS * groups) + place


def packed_row(values, sums, groups):
    at, sums_at = slots(KINDS, groups)
    lane = lax.broadcasted_iota(jnp.int32, (KINDS, LANES), 1)
    kind = lax.broadcasted_iota(jnp.int32, (KINDS, LANES), 0)
    row = jnp.where(lane == at + kind, jnp.broadcast_to(values, lane.shape), 0.0)
    for n, value in enumerate(sums):
        here = (lane == sums_at + n) & (kind == 0)
        row = jnp.where(here, jnp.broadcast_to(value, lane.shape), row)
    return jnp.sum(row, axis=0, keepdims=True)


def restrict(weights, field, modes):
    return jnp.sum(mm(weights, field) * modes, axis=1, keepdims=True)


def unpack(packed, coarse, count):
    half = packed.shape[0] // 2
    even = packed[pl.ds(0, half, stride=2), :]
    odd = packed[pl.ds(1, half, stride=2), :]
    lane = lax.broadcasted_iota(jnp.int32, (half, LANES), 1)
    low = lane < LANES // 2
    coarse[...] = jnp.where(low, even, odd)
    sums = jnp.sum(jnp.where(low, odd, even), axis=0, keepdims=True)
    kind = lax.rem(lax.broadcasted_iota(jnp.int32, (1, LANES), 1), KINDS)
    return [
        jnp.sum(jnp.where(kind == n, sums, 0.0), axis=1, keepdims=True) for n in range(count)
    ]


def solve_coarse(coarse, own, low, high):
    tiles = coarse.shape[0]
    parts = [[], [], []]
    for group in range(0, tiles, 8):
        partial = [None, None, None]
        for j in range(group, min(group + 8, tiles)):
            vector = jnp.broadcast_to(coarse[pl.ds(j, 1), :], (KINDS, LANES))
            for n, block in enumerate(
                (
                    own[:, j * LANES : (j + 1) * LANES],
                    low[j * KINDS : (j + 1) * KINDS, :],
                    high[j * KINDS : (j + 1) * KINDS, :],
                )
            ):
                term = block * vector
                partial[n] = term if partial[n] is None else partial[n] + term
        for n in range(3):
            parts[n].append(partial[n])
    return [
        jnp.sum(functools.reduce(jnp.add, part), axis=1, keepdims=True) for part in parts
    ]


def at_rows(value, start, rows):
    pieces = [value]
    if start:
        pieces.insert(0, jnp.zeros((start, value.shape[1]), F32))
    rest = rows - start - value.shape[0]
    if rest:
        pieces.append(jnp.zeros((rest, value.shape[1]), F32))
    return jnp.concatenate(pieces, axis=0)


def lifted(field, terms):
    width = field.shape[1]
    head = field[:, :LANES]
    tail = field[:, width - LANES :]
    zeros = jnp.zeros((field.shape[0], FACE), F32)
    head = head + jnp.concatenate([terms[:, :FACE], zeros], axis=1)
    tail = tail + jnp.concatenate([zeros, terms[:, FACE:]], axis=1)
    return jnp.concatenate([head, field[:, LANES : width - LANES], tail], axis=1)


def start_kernel(
    groups,
    rhs,
    kappa,
    local_inverse,
    modes,
    coarse_weight,
    coarse_mask,
    coarse_inverse,
    neighbours,
    row,
    halo,
    local,
    columns,
    links,
    weights,
):
    count = rhs.shape[0]
    subdomain = lax.axis_index("sub") * groups + lax.axis_index("grp")
    base = subdomain * count
    c = coarse_weight[...] * coarse_mask[...].astype(F32)
    weights[...] = c
    field = rhs[...]
    values = restrict(c, field, modes[...])
    row[...] = jnp.broadcast_to(
        packed_row(values, [total(field * field)], groups), row.shape
    )

    named = neighbours[...]
    slot = lax.broadcasted_iota(jnp.int32, named.shape, 0)
    shift = jnp.where(slot == 2, -groups * count, jnp.where(slot == 3, groups * count, 0))
    inside = jnp.where(named >= 0, named - (base + shift), -1).astype(F32)
    stacked = jnp.concatenate(
        [
            inside,
            jnp.broadcast_to(kappa[...], (4, count)),
            c,
            jnp.zeros((LANES - 16, count), F32),
        ],
        axis=0,
    )
    turned = jnp.transpose(stacked)
    columns[...] = turned

    lane = lax.broadcasted_iota(jnp.int32, (count, count), 1)
    line = lax.broadcasted_iota(jnp.int32, (count, count), 0)
    spot = turned[:, :4].astype(jnp.int32)

    def named_by(n):
        return (lane == spot[:, n : n + 1]).astype(F32)

    degree = jnp.sum((turned[:, :4] >= 0.0).astype(F32), axis=1, keepdims=True)
    own = jnp.where(lane == line, degree, 0.0) - (named_by(0) + named_by(1))
    links[:, :count] = (-named_by(2)).astype(BF16)
    links[:, count : 2 * count] = own.astype(BF16)
    links[:, 2 * count :] = (-named_by(3)).astype(BF16)

    solved = mm(field, local_inverse[...]) / turned[:, 4:5]
    local[...] = solved

    tiles = coarse_inverse.shape[1] // LANES
    for j in range(tiles):
        halo[j * KINDS : (j + 1) * KINDS, :] = coarse_inverse[:, j * LANES : (j + 1) * LANES]
    at = tiles * KINDS
    halo[at : at + KINDS, :] = c[:, :LANES]
    halo[at + KINDS : at + 2 * KINDS, :] = c[:, LANES:]
    halo[at + 2 * KINDS :, :] = faces(solved)


def first_kernel(
    groups,
    packed,
    coarse_inverse,
    low,
    high,
    rhs,
    local,
    columns,
    links,
    weights,
    modes,
    stiffness,
    local_inverse,
    row,
    edge,
    z_one,
    w_one,
    next_local,
    beside,
    window,
    scalars,
    coarse,
):
    count = rhs.shape[0]
    square = unpack(packed, coarse, 1)[0]
    beta = jnp.sqrt(square)
    solved = [value / beta for value in solve_coarse(coarse, coarse_inverse, low, high)]
    m = modes[...]
    edges = faces(m)
    turned = columns[...]
    z = local[...] / beta + mm(turned, at_rows(solved[0] * m, 8, LANES))
    z_one[...] = z

    at = (coarse_inverse.shape[1] // LANES) * KINDS

    def weights_of(halo):
        return jnp.concatenate(
            [halo[at : at + KINDS, :], halo[at + KINDS : at + 2 * KINDS, :]], axis=1
        )

    sides = jnp.transpose(at_rows(jnp.concatenate([weights_of(low), weights_of(high)], axis=0), 0, LANES))
    beside[...] = sides
    window[:count, :] = low[at + 2 * KINDS :, :] / beta + mm(
        sides, at_rows(solved[1] * edges, 0, LANES)
    )
    window[count : 2 * count, :] = faces(z)
    window[2 * count :, :] = high[at + 2 * KINDS :, :] / beta + mm(
        sides, at_rows(solved[2] * edges, 8, LANES)
    )
    penalty = SIGMA * exact_left(links[...], window[...])
    kappa = turned[:, 4:5]
    w = lifted(kappa * mm(z, stiffness[...]), penalty)
    w_one[...] = w
    values = restrict(weights[...], w, m)
    sums = [total(w * (rhs[...] / beta)), total(w * w)]
    row[...] = jnp.broadcast_to(packed_row(values, sums, groups), row.shape)
    following = mm(w, local_inverse[...]) / kappa
    next_local[...] = following
    edge[...] = faces(following)
    scalars[...] = jnp.broadcast_to(beta, scalars.shape)


def second_kernel(
    packed,
    coarse_inverse,
    low,
    high,
    low_edge,
    high_edge,
    rhs,
    local,
    columns,
    links,
    modes,
    stiffness,
    beside,
    window,
    z_one,
    w_one,
    scalars,
    row,
    z_two,
    carried,
    coarse,
    frame,
):
    count = rhs.shape[0]
    h11, s_one = unpack(packed, coarse, 2)
    beta = scalars[:1, :1]
    h21 = jnp.sqrt(s_one - h11 * h11)
    solved = solve_coarse(coarse, coarse_inverse, low, high)
    m = modes[...]
    edges = faces(m)
    turned = columns[...]
    sides = beside[...]
    z = local[...] + mm(turned, at_rows(solved[0] * m, 8, LANES))
    z = (z - h11 * z_one[...]) / h21
    z_two[...] = z
    frame[:count, :] = low_edge[...] + mm(sides, at_rows(solved[1] * edges, 0, LANES))
    frame[2 * count :, :] = high_edge[...] + mm(sides, at_rows(solved[2] * edges, 8, LANES))
    frame[:count, :] = (frame[:count, :] - h11 * window[:count, :]) / h21
    frame[2 * count :, :] = (frame[2 * count :, :] - h11 * window[2 * count :, :]) / h21
    frame[count : 2 * count, :] = faces(z)
    penalty = SIGMA * exact_left(links[...], frame[...])
    w = lifted(turned[:, 4:5] * mm(z, stiffness[...]), penalty)
    first = rhs[...] / beta
    second = (w_one[...] - h11 * first) / h21
    lane = lax.broadcasted_iota(jnp.int32, (1, LANES), 1)
    sums = jnp.zeros((1, LANES), F32)
    for n, value in enumerate((total(w * first), total(w * second), total(w * w))):
        sums = jnp.where(lane == n, jnp.broadcast_to(value, sums.shape), sums)
    row[...] = jnp.broadcast_to(sums, row.shape)
    keep = jnp.zeros((1, LANES), F32)
    for n, value in enumerate((beta, h11, s_one, h21)):
        keep = jnp.where(lane == n, jnp.broadcast_to(value, keep.shape), keep)
    carried[...] = jnp.broadcast_to(keep, carried.shape)


def last_kernel(packed, carried, z_one, z_two, out):
    sums = jnp.sum(packed[...], axis=0, keepdims=True)
    h12, h22, s_two = sums[:, 0:1], sums[:, 1:2], sums[:, 2:3]
    kept = carried[:1, :]
    beta, h11, s_one, h21 = (kept[:, n : n + 1] for n in range(4))
    cross = h11 * h12 + h21 * h22
    det = s_one * s_two - cross * cross
    y_one = beta * (h11 * s_two - h12 * cross) / det
    y_two = beta * (h12 * s_one - h11 * cross) / det
    out[...] = y_one * z_one[...] + y_two * z_two[...]


def fan_kernel(rows, out):
    out[...] = jnp.broadcast_to(jnp.sum(rows[...], axis=0, keepdims=True), out.shape)


def body(
    rhs,
    kappa,
    stiffness,
    local_inverse,
    modes,
    coarse_weight,
    coarse_mask,
    coarse_inverse,
    neighbours,
    interpret=False,
):
    count, width = rhs.shape
    groups = lax.axis_size("grp")
    lines = lax.axis_size("sub")
    tall = coarse_inverse.shape[1] // LANES * KINDS + 2 * KINDS + count
    params = pltpu.CompilerParams(vmem_limit_bytes=40 * 1024 * 1024)

    def call(kernel, outs, name, scratch=()):
        return pl.pallas_call(
            kernel,
            out_shape=outs,
            scratch_shapes=list(scratch),
            compiler_params=params,
            name=name,
            interpret=interpret,
        )

    def array(*shape, dtype=F32):
        return jax.ShapeDtypeStruct(shape, dtype)

    def everywhere(row):
        own = lax.all_to_all(row.reshape(groups, 1, LANES), "grp", 0, 0, tiled=True)
        spread = call(fan_kernel, array(lines, LANES), "fan")(own.reshape(groups, LANES))
        every = lax.all_to_all(spread.reshape(lines, 1, LANES), "sub", 0, 0, tiled=True)
        return every.reshape(lines, LANES)

    up = [(i, i + 1) for i in range(lines - 1)]
    down = [(b, a) for a, b in up]

    def exchanged(block):
        return lax.ppermute(block, "sub", up), lax.ppermute(block, "sub", down)

    row, halo, local, columns, links, weights = call(
        functools.partial(start_kernel, groups),
        (
            array(groups, LANES),
            array(tall, LANES),
            array(count, width),
            array(count, LANES),
            array(count, 3 * count, dtype=BF16),
            array(KINDS, count),
        ),
        "start",
    )(
        rhs,
        kappa.reshape(1, count),
        local_inverse,
        modes,
        coarse_weight,
        coarse_mask,
        coarse_inverse,
        neighbours,
    )
    low, high = exchanged(halo)
    packed = everywhere(row)
    row, edge, z_one, w_one, following, beside, window, scalars = call(
        functools.partial(first_kernel, groups),
        (
            array(groups, LANES),
            array(count, LANES),
            array(count, width),
            array(count, width),
            array(count, width),
            array(count, LANES),
            array(3 * count, LANES),
            array(KINDS, LANES),
        ),
        "first",
        [pltpu.VMEM((lines // 2, LANES), F32)],
    )(
        packed,
        coarse_inverse,
        low,
        high,
        rhs,
        local,
        columns,
        links,
        weights,
        modes,
        stiffness,
        local_inverse,
    )
    low_edge, high_edge = exchanged(edge)
    packed = everywhere(row)
    row, z_two, carried = call(
        second_kernel,
        (array(groups, LANES), array(count, width), array(KINDS, LANES)),
        "second",
        [pltpu.VMEM((lines // 2, LANES), F32), pltpu.VMEM((3 * count, LANES), F32)],
    )(
        packed,
        coarse_inverse,
        low,
        high,
        low_edge,
        high_edge,
        rhs,
        following,
        columns,
        links,
        modes,
        stiffness,
        beside,
        window,
        z_one,
        w_one,
        scalars,
    )
    packed = everywhere(row)
    return call(last_kernel, array(count, width), "last")(packed, carried, z_one, z_two)


def solution(mesh, interpret=False):
    placed = (
        P(("sub", "grp"), None),
        P(("sub", "grp")),
        P(),
        P(),
        P(),
        P(None, ("sub", "grp")),
        P(None, ("sub", "grp")),
        P(("sub", "grp"), None),
        P(None, ("sub", "grp")),
    )
    return jax.shard_map(
        functools.partial(body, interpret=interpret),
        mesh=mesh,
        in_specs=placed,
        out_specs=P(("sub", "grp"), None),
        check_vma=False,
    )
```
